32 devices in a mesh: row: 4 (over z), col: 2 (over x), rep: 4 (over y, core).
Axes of the slice: x: 2, y: 2, z: 4, core: 2. Of those that a mesh axis runs over, the one named last changes fastest.
Arguments:
- density: bfloat16 [1536, 1536], P('row', 'col'), as said below
- keep_square: int32 [12, 12], P('row', 'col'), may hold values 0 or 1
- keep_cube: int32 [12, 12], P('row', 'col'), may hold values 0 or 1
Outputs:
- purified: float32 [1536, 1536], P(('row', 'rep'), 'col')
The draws below stay inside these ranges and needn't reach their ends.
Inputs may be any that keep to these rules, and one draw needn't show every extreme that they name: density is symmetric; its 128 x 128 diagonal blocks are always occupied, any other block may be zero or occupied at any distance from the diagonal.
All inputs are finite; a program needn't handle non-finite values. No bound on the sum of `keep_square` or of `keep_cube` on one device may be relied on, other than what follows from the above.
Results may differ from the reference program's by a relative error of at most 0.002.
Values may be sent and summed in bfloat16 or wider, within the bound.
A program may use at most 64 MiB of HBM per device.

```python
import jax
import jax.numpy as jnp

BLK = 128
MAT = 1536
NBLK = 12


def draw_density(key, part):
    block_count = MAT // BLK
    key_bits, key_values = jax.random.split(jax.random.fold_in(key, 17), 2)
    raw_bits = jax.random.randint(key_bits, (block_count, block_count), 0, 4)
    upper = jnp.triu((raw_bits == 0).astype(jnp.int32), 1)
    pattern = upper + upper.T + jnp.eye(block_count, dtype=jnp.int32) > 0
    blocks = jnp.broadcast_to(pattern.astype(jnp.float32)[:, None, :, None], (block_count, BLK, block_count, BLK)).reshape(MAT, MAT)
    values = jax.random.normal(key_values, (MAT, MAT), jnp.float32)
    values = (values + values.T) * 0.7071
    return (values * blocks * ((block_count // 4 + 1) * BLK * 1.0) ** (-0.25)).astype(jnp.bfloat16)


def plant(result, key, low, top_value):
    index_at = [jax.random.randint(jax.random.fold_in(key, axis), (), 0, length) for axis, length in enumerate(result.shape)]
    widest = result.shape.index(max(result.shape))
    next_to = index_at[:widest] + [(index_at[widest] + 1) % result.shape[widest]] + index_at[widest + 1:]
    return result.at[tuple(index_at)].set(low).at[tuple(next_to)].set(top_value)


def setup_inputs(seed: int = 0) -> dict:
    keys = jax.random.split(jax.random.key(seed), 4)
    density = draw_density(jax.random.fold_in(keys[3], 71), 0)
    keep_square = plant((jax.random.randint(keys[1], (NBLK, NBLK), 0, 4) < 3).astype(jnp.int32), jax.random.fold_in(keys[1], 1), 0, 1)
    keep_cube = plant((jax.random.randint(keys[2], (NBLK, NBLK), 0, 4) < 3).astype(jnp.int32), jax.random.fold_in(keys[2], 1), 0, 1)
    return dict(density=density, keep_square=keep_square, keep_cube=keep_cube)


def widen(mask):
    count = mask.shape[0]
    blocks = jnp.broadcast_to(mask.astype(jnp.float32)[:, None, :, None], (count, BLK, count, BLK))
    return blocks.reshape(count * BLK, count * BLK)


def reference(density, keep_square, keep_cube):
    square = jnp.dot(density, density, preferred_element_type=jnp.float32) * widen(keep_square)
    square_low = square.astype(jnp.bfloat16)
    cube = jnp.dot(square_low, density, preferred_element_type=jnp.float32) * widen(keep_cube)
    return 3.0 * square - 2.0 * cube
```

```python
import functools

import jax
import jax.numpy as jnp
from jax import lax
from jax.experimental import pallas as pl
from jax.experimental.pallas import tpu as pltpu
from jax.sharding import PartitionSpec as P

MESH = pl.DeviceIdType.MESH


def flip(index, bit):
    return index + bit - 2 * bit * (index // bit % 2)


def kernel(rows, cols, reps, block, chunks, density, keep_square, keep_cube, out,
           panel, left, low, total, z_send, z_recv, r_send, r_recv, a_send, a_recv,
           l_send, l_recv, local_sem):
    tile_rows, tile_cols = density.shape
    own = tile_rows // reps
    piece = own // chunks
    ratio = tile_cols // tile_rows
    z, c, p = lax.axis_index("row"), lax.axis_index("col"), lax.axis_index("rep")
    bits = []
    bit = reps // 2
    while bit:
        bits.append(bit)
        bit //= 2
    others = [lax.rem(c + step, cols) for step in range(1, cols)]

    barrier = pltpu.get_barrier_semaphore()
    for step, ok in ((1, z < rows - 1), (-1, z > 0)):
        @pl.when(ok)
        def _():
            pl.semaphore_signal(barrier, inc=1, device_id={"row": z + step}, device_id_type=MESH)
    for bit in bits:
        pl.semaphore_signal(barrier, inc=1, device_id={"rep": flip(p, bit)}, device_id_type=MESH)
    for other in others:
        pl.semaphore_signal(barrier, inc=1, device_id={"col": other}, device_id_type=MESH)
    keep_tile = pltpu.make_async_copy(
        density, panel.at[pl.ds(pl.multiple_of(z * tile_rows, tile_rows), tile_rows)], local_sem.at[0])
    keep_tile.start()
    keep_left = [
        pltpu.make_async_copy(
            density.at[pl.ds(pl.multiple_of(p * own, own), own), pl.ds(part * tile_rows, tile_rows)],
            left.at[c * ratio + part], local_sem.at[1 + part])
        for part in range(ratio)
    ]
    for copy in keep_left:
        copy.start()
    below, above = (z + rows - 1) // rows, (2 * rows - 2 - z) // rows
    pl.semaphore_wait(barrier, len(bits) + len(others) + below + above)

    def slot(t, member, q):
        return panel.at[pl.ds(pl.multiple_of(t * tile_rows + member * own + q * piece, piece), piece)]

    def z_copy(t, q, step, first=False):
        source = slot(t, p, q)
        if first:
            source = density.at[pl.ds(pl.multiple_of(p * own + q * piece, piece), piece)]
        return pltpu.make_async_remote_copy(
            source, slot(t, p, q), z_send.at[(step + 1) // 2, t, q], z_recv.at[t, q],
            device_id={"row": z + step}, device_id_type=MESH)

    def r_copies(t, q, stage):
        members = [p]
        for bit in bits[:stage]:
            members = members + [flip(member, bit) for member in members]
        peer = flip(p, bits[stage])
        base = 2 ** stage - 1
        return [
            pltpu.make_async_remote_copy(
                slot(t, member, q), slot(t, member, q), r_send.at[base + i, t, q],
                r_recv.at[base + i, t, q], device_id={"rep": peer}, device_id_type=MESH)
            for i, member in enumerate(members)
        ]

    def r_waits(t, q, stage):
        peer = flip(p, bits[stage])
        members = [peer]
        for bit in bits[:stage]:
            members = members + [flip(member, bit) for member in members]
        base = 2 ** stage - 1
        for i, member in enumerate(members):
            pltpu.make_async_remote_copy(
                slot(t, member, q), slot(t, member, q), r_send.at[base + i, t, q],
                r_recv.at[base + i, t, q], device_id={"rep": peer}, device_id_type=MESH).wait_recv()

    def a_copy(owner, peer, part):
        return pltpu.make_async_remote_copy(
            density.at[pl.ds(pl.multiple_of(p * own, own), own), pl.ds(part * tile_rows, tile_rows)],
            left.at[owner * ratio + part], a_send.at[peer, part], a_recv.at[owner, part],
            device_id={"col": peer}, device_id_type=MESH)

    def l_copy(owner, peer, part):
        return pltpu.make_async_remote_copy(
            low.at[owner * ratio + part], low.at[owner * ratio + part],
            l_send.at[peer, part], l_recv.at[owner, part],
            device_id={"col": peer}, device_id_type=MESH)

    ways = ((1, z < rows - 1), (-1, z > 0))
    for q in range(chunks):
        for step, ok in ways:
            @pl.when(ok)
            def _():
                z_copy(z, q, step, True).start()
    for other in others:
        for part in range(ratio):
            a_copy(c, other, part).start()

    def arrivals(distance):
        return ((1, z - distance, z - distance >= 0, z < rows - 1),
                (-1, z + distance, z + distance < rows, z > 0))

    def take(distance):
        for q in range(chunks):
            for step, t, ok, onward in arrivals(distance):
                @pl.when(ok)
                def _():
                    z_copy(t, q, step).wait_recv()

                    @pl.when(onward)
                    def _():
                        z_copy(t, q, step).start()
                    for copy in r_copies(t, q, 0):
                        copy.start()

    def spread(distance, stage):
        for q in range(chunks):
            for step, t, ok, onward in arrivals(distance):
                @pl.when(ok)
                def _():
                    r_waits(t, q, stage - 1)
                    for copy in r_copies(t, q, stage):
                        copy.start()

    def product(factor, t):
        return jnp.dot(factor[t], panel[pl.ds(pl.multiple_of(t * tile_rows, tile_rows), tile_rows), :],
                       preferred_element_type=jnp.float32)

    def use(distance):
        for step, t, ok, onward in arrivals(distance):
            @pl.when(ok)
            def _():
                for q in range(chunks):
                    r_waits(t, q, len(bits) - 1)
                total[...] += product(left, t)

    keep_tile.wait()
    for copy in keep_left:
        copy.wait()
    started = False
    for distance in range(1, rows + len(bits)):
        if distance < rows:
            take(distance)
        for stage in range(1, len(bits)):
            if 1 <= distance - stage < rows:
                spread(distance - stage, stage)
        if not started:
            for other in others:
                for part in range(ratio):
                    a_copy(other, other, part).wait_recv()
            total[...] = product(left, z)
            started = True
        if 1 <= distance - len(bits) < rows:
            use(distance - len(bits))

    row_block = (p * own + lax.broadcasted_iota(jnp.int32, (own, block), 0)) // block

    def widen(keep, column):
        wide = jnp.zeros((own, block), jnp.float32)
        for i in range(tile_rows // block):
            wide = jnp.where(row_block == i, keep[i, column].astype(jnp.float32), wide)
        return wide

    per_part = tile_rows // block
    for column in range(tile_cols // block):
        span = pl.ds(column * block, block)
        square = total[:, span] * widen(keep_square, column)
        total[:, span] = square
        low[c * ratio + column // per_part, :, pl.ds(column % per_part * block, block)] = square.astype(jnp.bfloat16)
    for other in others:
        for part in range(ratio):
            l_copy(c, other, part).start()
    cube = product(low, c * ratio)
    for part in range(1, ratio):
        cube = cube + product(low, c * ratio + part)
    out[...] = cube
    for other in others:
        for part in range(ratio):
            l_copy(other, other, part).wait_recv()
            out[...] += product(low, other * ratio + part)
    for column in range(tile_cols // block):
        span = pl.ds(column * block, block)
        out[:, span] = 3.0 * total[:, span] - 2.0 * (out[:, span] * widen(keep_cube, column))

    for q in range(chunks):
        for step, ok in ways:
            @pl.when(ok)
            def _():
                z_copy(z, q, step, True).wait_send()
        for distance in range(1, rows):
            for step, t, ok, onward in arrivals(distance):
                @pl.when(ok)
                def _():
                    @pl.when(onward)
                    def _():
                        z_copy(t, q, step).wait_send()
                    for stage in range(len(bits)):
                        for copy in r_copies(t, q, stage):
                            copy.wait_send()
    for other in others:
        for part in range(ratio):
            a_copy(c, other, part).wait_send()
            l_copy(c, other, part).wait_send()


def local(rows, cols, reps, mat, density, keep_square, keep_cube):
    tile_rows, tile_cols = density.shape
    block = tile_rows // keep_square.shape[0]
    own = tile_rows // reps
    ratio = tile_cols // tile_rows
    chunks = 2 if own % 32 == 0 else 1
    dma = pltpu.SemaphoreType.DMA
    return pl.pallas_call(
        functools.partial(kernel, rows, cols, reps, block, chunks),
        out_shape=jax.ShapeDtypeStruct((own, tile_cols), jnp.float32),
        in_specs=[
            pl.BlockSpec(memory_space=pl.ANY),
            pl.BlockSpec(memory_space=pltpu.SMEM),
            pl.BlockSpec(memory_space=pltpu.SMEM),
        ],
        out_specs=pl.BlockSpec(memory_space=pltpu.VMEM),
        scratch_shapes=[
            pltpu.VMEM((mat, tile_cols), jnp.bfloat16),
            pltpu.VMEM((rows, own, tile_rows), jnp.bfloat16),
            pltpu.VMEM((rows, own, tile_rows), jnp.bfloat16),
            pltpu.VMEM((own, tile_cols), jnp.float32),
            dma((2, rows, chunks)),
            dma((rows, chunks)),
            dma((reps - 1, rows, chunks)),
            dma((reps - 1, rows, chunks)),
            dma((cols, ratio)),
            dma((cols, ratio)),
            dma((cols, ratio)),
            dma((cols, ratio)),
            dma((1 + ratio,)),
        ],
        compiler_params=pltpu.CompilerParams(collective_id=0, has_side_effects=True),
    )(density, keep_square, keep_cube)


def solution(mesh):
    rows, cols, reps = (mesh.shape[axis] for axis in ("row", "col", "rep"))

    def body(density, keep_square, keep_cube):
        return local(rows, cols, reps, density.shape[0] * rows, density, keep_square, keep_cube)

    return jax.shard_map(
        body,
        mesh=mesh,
        in_specs=(P("row", "col"), P("row", "col"), P("row", "col")),
        out_specs=P(("row", "rep"), "col"),
        check_vma=False,
    )
```

```python
import functools

import jax
import jax.numpy as jnp
from jax import lax
from jax.experimental import pallas as pl
from jax.experimental.pallas import tpu as pltpu
from jax.sharding import PartitionSpec as P

MESH = pl.DeviceIdType.MESH


def flip(index, bit):
    return index + bit - 2 * bit * (index // bit % 2)


def kernel(rows, cols, reps, block, chunks, density, keep_square, keep_cube, out,
           panel, left, low, total, z_send, z_recv, r_send, r_recv, a_send, a_recv,
           l_send, l_recv, local_sem):
    tile_rows, tile_cols = density.shape
    own = tile_rows // reps
    piece = own // chunks
    ratio = tile_cols // tile_rows
    z, c, p = lax.axis_index("row"), lax.axis_index("col"), lax.axis_index("rep")
    bits = []
    bit = reps // 2
    while bit:
        bits.append(bit)
        bit //= 2
    others = [lax.rem(c + step, cols) for step in range(1, cols)]

    barrier = pltpu.get_barrier_semaphore()
    for step, ok in ((1, z < rows - 1), (-1, z > 0)):
        @pl.when(ok)
        def _():
            pl.semaphore_signal(barrier, inc=1, device_id={"row": z + step}, device_id_type=MESH)
    for bit in bits:
        pl.semaphore_signal(barrier, inc=1, device_id={"rep": flip(p, bit)}, device_id_type=MESH)
    for other in others:
        pl.semaphore_signal(barrier, inc=1, device_id={"col": other}, device_id_type=MESH)
    keep_tile = pltpu.make_async_copy(
        density, panel.at[pl.ds(pl.multiple_of(z * tile_rows, tile_rows), tile_rows)], local_sem.at[0])
    keep_tile.start()
    keep_left = [
        pltpu.make_async_copy(
            density.at[pl.ds(pl.multiple_of(p * own, own), own), pl.ds(part * tile_rows, tile_rows)],
            left.at[c * ratio + part], local_sem.at[1 + part])
        for part in range(ratio)
    ]
    for copy in keep_left:
        copy.start()
    below, above = (z + rows - 1) // rows, (2 * rows - 2 - z) // rows
    pl.semaphore_wait(barrier, len(bits) + len(others) + below + above)

    def slot(t, member, q):
        return panel.at[pl.ds(pl.multiple_of(t * tile_rows + member * own + q * piece, piece), piece)]

    def z_copy(t, q, step, first=False):
        source = slot(t, p, q)
        if first:
            source = density.at[pl.ds(pl.multiple_of(p * own + q * piece, piece), piece)]
        return pltpu.make_async_remote_copy(
            source, slot(t, p, q), z_send.at[(step + 1) // 2, t, q], z_recv.at[t, q],
            device_id={"row": z + step}, device_id_type=MESH)

    def r_copies(t, q, stage):
        members = [p]
        for bit in bits[:stage]:
            members = members + [flip(member, bit) for member in members]
        peer = flip(p, bits[stage])
        base = 2 ** stage - 1
        return [
            pltpu.make_async_remote_copy(
                slot(t, member, q), slot(t, member, q), r_send.at[base + i, t, q],
                r_recv.at[base + i, t, q], device_id={"rep": peer}, device_id_type=MESH)
            for i, member in enumerate(members)
        ]

    def r_waits(t, q, stage):
        peer = flip(p, bits[stage])
        members = [peer]
        for bit in bits[:stage]:
            members = members + [flip(member, bit) for member in members]
        base = 2 ** stage - 1
        for i, member in enumerate(members):
            pltpu.make_async_remote_copy(
                slot(t, member, q), slot(t, member, q), r_send.at[base + i, t, q],
                r_recv.at[base + i, t, q], device_id={"rep": peer}, device_id_type=MESH).wait_recv()

    def a_copy(owner, peer, part):
        return pltpu.make_async_remote_copy(
            density.at[pl.ds(pl.multiple_of(p * own, own), own), pl.ds(part * tile_rows, tile_rows)],
            left.at[owner * ratio + part], a_send.at[peer, part], a_recv.at[owner, part],
            device_id={"col": peer}, device_id_type=MESH)

    def l_copy(owner, peer, part):
        return pltpu.make_async_remote_copy(
            low.at[owner * ratio + part], low.at[owner * ratio + part],
            l_send.at[peer, part], l_recv.at[owner, part],
            device_id={"col": peer}, device_id_type=MESH)

    ways = ((1, z < rows - 1), (-1, z > 0))
    for q in range(chunks):
        for step, ok in ways:
            @pl.when(ok)
            def _():
                z_copy(z, q, step, True).start()
    for other in others:
        for part in range(ratio):
            a_copy(c, other, part).start()

    def arrivals(distance):
        return ((1, z - distance, z - distance >= 0, z < rows - 1),
                (-1, z + distance, z + distance < rows, z > 0))

    def take(distance):
        for q in range(chunks):
            for step, t, ok, onward in arrivals(distance):
                @pl.when(ok)
                def _():
                    z_copy(t, q, step).wait_recv()

                    @pl.when(onward)
                    def _():
                        z_copy(t, q, step).start()
                    for copy in r_copies(t, q, 0):
                        copy.start()

    def spread(distance, stage):
        for q in range(chunks):
            for step, t, ok, onward in arrivals(distance):
                @pl.when(ok)
                def _():
                    r_waits(t, q, stage - 1)
                    for copy in r_copies(t, q, stage):
                        copy.start()

    def product(factor, t):
        return jnp.dot(factor[t], panel[pl.ds(pl.multiple_of(t * tile_rows, tile_rows), tile_rows), :],
                       preferred_element_type=jnp.float32)

    def use(distance):
        for step, t, ok, onward in arrivals(distance):
            @pl.when(ok)
            def _():
                for q in range(chunks):
                    r_waits(t, q, len(bits) - 1)
                total[...] += product(left, t)

    keep_tile.wait()
    for copy in keep_left:
        copy.wait()
    started = False
    for distance in range(1, rows + len(bits)):
        if distance < rows:
            take(distance)
        for stage in range(1, len(bits)):
            if 1 <= distance - stage < rows:
                spread(distance - stage, stage)
        if not started:
            for other in others:
                for part in range(ratio):
                    a_copy(other, other, part).wait_recv()
            total[...] = product(left, z)
            started = True
        if 1 <= distance - len(bits) < rows:
            use(distance - len(bits))

    row_block = (p * own + lax.broadcasted_iota(jnp.int32, (own, block), 0)) // block

    def widen(keep, column):
        wide = jnp.zeros((own, block), jnp.float32)
        for i in range(tile_rows // block):
            wide = jnp.where(row_block == i, keep[i, column].astype(jnp.float32), wide)
        return wide

    per_part = tile_rows // block
    for column in range(tile_cols // block):
        span = pl.ds(column * block, block)
        square = total[:, span] * widen(keep_square, column)
        total[:, span] = square
        low[c * ratio + column // per_part, :, pl.ds(column % per_part * block, block)] = square.astype(jnp.bfloat16)
    for other in others:
        for part in range(ratio):
            l_copy(c, other, part).start()
    cube = product(low, c * ratio)
    for part in range(1, ratio):
        cube = cube + product(low, c * ratio + part)
    out[...] = cube
    for other in others:
        for part in range(ratio):
            l_copy(other, other, part).wait_recv()
            out[...] += product(low, other * ratio + part)
    for column in range(tile_cols // block):
        span = pl.ds(column * block, block)
        out[:, span] = 3.0 * total[:, span] - 2.0 * (out[:, span] * widen(keep_cube, column))

    for q in range(chunks):
        for step, ok in ways:
            @pl.when(ok)
            def _():
                z_copy(z, q, step, True).wait_send()
        for distance in range(1, rows):
            for step, t, ok, onward in arrivals(distance):
                @pl.when(ok)
                def _():
                    @pl.when(onward)
                    def _():
                        z_copy(t, q, step).wait_send()
                    for stage in range(len(bits)):
                        for copy in r_copies(t, q, stage):
                            copy.wait_send()
    for other in others:
        for part in range(ratio):
            a_copy(c, other, part).wait_send()
            l_copy(c, other, part).wait_send()


def local(rows, cols, reps, mat, density, keep_square, keep_cube):
    tile_rows, tile_cols = density.shape
    block = tile_rows // keep_square.shape[0]
    own = tile_rows // reps
    ratio = tile_cols // tile_rows
    chunks = 3 if own % 48 == 0 else 1
    dma = pltpu.SemaphoreType.DMA
    return pl.pallas_call(
        functools.partial(kernel, rows, cols, reps, block, chunks),
        out_shape=pltpu.VMEM((own, tile_cols), jnp.float32),
        in_specs=[
            pl.BlockSpec(memory_space=pl.ANY),
            pl.BlockSpec(memory_space=pltpu.SMEM),
            pl.BlockSpec(memory_space=pltpu.SMEM),
        ],
        out_specs=pl.BlockSpec(memory_space=pltpu.VMEM),
        scratch_shapes=[
            pltpu.VMEM((mat, tile_cols), jnp.bfloat16),
            pltpu.VMEM((rows, own, tile_rows), jnp.bfloat16),
            pltpu.VMEM((rows, own, tile_rows), jnp.bfloat16),
            pltpu.VMEM((own, tile_cols), jnp.float32),
            dma((2, rows, chunks)),
            dma((rows, chunks)),
            dma((reps - 1, rows, chunks)),
            dma((reps - 1, rows, chunks)),
            dma((cols, ratio)),
            dma((cols, ratio)),
            dma((cols, ratio)),
            dma((cols, ratio)),
            dma((1 + ratio,)),
        ],
        compiler_params=pltpu.CompilerParams(collective_id=0, has_side_effects=True),
    )(density, keep_square, keep_cube)


def solution(mesh):
    rows, cols, reps = (mesh.shape[axis] for axis in ("row", "col", "rep"))

    def body(density, keep_square, keep_cube):
        return local(rows, cols, reps, density.shape[0] * rows, density, keep_square, keep_cube)

    return jax.shard_map(
        body,
        mesh=mesh,
        in_specs=(P("row", "col"), P("row", "col"), P("row", "col")),
        out_specs=P(("row", "rep"), "col"),
        check_vma=False,
    )
```

```python
import functools

import jax
import jax.numpy as jnp
from jax import lax
from jax.experimental import pallas as pl
from jax.experimental.pallas import tpu as pltpu
from jax.sharding import PartitionSpec as P

MESH = pl.DeviceIdType.MESH


def flip(index, bit):
    return index + bit - 2 * bit * (index // bit % 2)


def kernel(rows, cols, reps, block, chunks, density, keep_square, keep_cube, out,
           panel, left, low, total, z_send, z_recv, r_send, r_recv, a_send, a_recv,
           l_send, l_recv, local_sem):
    tile_rows, tile_cols = density.shape
    own = tile_rows // reps
    piece = own // chunks
    ratio = tile_cols // tile_rows
    z, c, p = lax.axis_index("row"), lax.axis_index("col"), lax.axis_index("rep")
    bits = []
    bit = reps // 2
    while bit:
        bits.append(bit)
        bit //= 2
    others = [lax.rem(c + step, cols) for step in range(1, cols)]

    barrier = pltpu.get_barrier_semaphore()
    for step, ok in ((1, z < rows - 1), (-1, z > 0)):
        @pl.when(ok)
        def _():
            pl.semaphore_signal(barrier, inc=1, device_id={"row": z + step}, device_id_type=MESH)
    for bit in bits:
        pl.semaphore_signal(barrier, inc=1, device_id={"rep": flip(p, bit)}, device_id_type=MESH)
    for other in others:
        pl.semaphore_signal(barrier, inc=1, device_id={"col": other}, device_id_type=MESH)
    keep_tile = pltpu.make_async_copy(
        density, panel.at[pl.ds(pl.multiple_of(z * tile_rows, tile_rows), tile_rows)], local_sem.at[0])
    keep_tile.start()
    keep_left = [
        pltpu.make_async_copy(
            density.at[pl.ds(pl.multiple_of(p * own, own), own), pl.ds(part * tile_rows, tile_rows)],
            left.at[c * ratio + part], local_sem.at[1 + part])
        for part in range(ratio)
    ]
    for copy in keep_left:
        copy.start()
    below, above = (z + rows - 1) // rows, (2 * rows - 2 - z) // rows
    pl.semaphore_wait(barrier, len(bits) + len(others) + below + above)

    def slot(t, member, q):
        return panel.at[pl.ds(pl.multiple_of(t * tile_rows + member * own + q * piece, piece), piece)]

    def z_copy(t, q, step, first=False):
        source = slot(t, p, q)
        if first:
            source = density.at[pl.ds(pl.multiple_of(p * own + q * piece, piece), piece)]
        return pltpu.make_async_remote_copy(
            source, slot(t, p, q), z_send.at[(step + 1) // 2, t, q], z_recv.at[t, q],
            device_id={"row": z + step}, device_id_type=MESH)

    def r_copies(t, q, stage):
        members = [p]
        for bit in bits[:stage]:
            members = members + [flip(member, bit) for member in members]
        peer = flip(p, bits[stage])
        base = 2 ** stage - 1
        return [
            pltpu.make_async_remote_copy(
                slot(t, member, q), slot(t, member, q), r_send.at[base + i, t, q],
                r_recv.at[base + i, t, q], device_id={"rep": peer}, device_id_type=MESH)
            for i, member in enumerate(members)
        ]

    def r_waits(t, q, stage):
        peer = flip(p, bits[stage])
        members = [peer]
        for bit in bits[:stage]:
            members = members + [flip(member, bit) for member in members]
        base = 2 ** stage - 1
        for i, member in enumerate(members):
            pltpu.make_async_remote_copy(
                slot(t, member, q), slot(t, member, q), r_send.at[base + i, t, q],
                r_recv.at[base + i, t, q], device_id={"rep": peer}, device_id_type=MESH).wait_recv()

    def a_copy(owner, peer, part):
        return pltpu.make_async_remote_copy(
            density.at[pl.ds(pl.multiple_of(p * own, own), own), pl.ds(part * tile_rows, tile_rows)],
            left.at[owner * ratio + part], a_send.at[peer, part], a_recv.at[owner, part],
            device_id={"col": peer}, device_id_type=MESH)

    def l_copy(owner, peer, part):
        return pltpu.make_async_remote_copy(
            low.at[owner * ratio + part], low.at[owner * ratio + part],
            l_send.at[peer, part], l_recv.at[owner, part],
            device_id={"col": peer}, device_id_type=MESH)

    ways = ((1, z < rows - 1), (-1, z > 0))
    for q in range(chunks):
        for step, ok in ways:
            @pl.when(ok)
            def _():
                z_copy(z, q, step, True).start()
    for other in others:
        for part in range(ratio):
            a_copy(c, other, part).start()

    def arrivals(distance):
        return ((1, z - distance, z - distance >= 0, z < rows - 1),
                (-1, z + distance, z + distance < rows, z > 0))

    def take(distance):
        for q in range(chunks):
            for step, t, ok, onward in arrivals(distance):
                @pl.when(ok)
                def _():
                    z_copy(t, q, step).wait_recv()

                    @pl.when(onward)
                    def _():
                        z_copy(t, q, step).start()
                    for copy in r_copies(t, q, 0):
                        copy.start()

    def spread(distance, stage):
        for q in range(chunks):
            for step, t, ok, onward in arrivals(distance):
                @pl.when(ok)
                def _():
                    r_waits(t, q, stage - 1)
                    for copy in r_copies(t, q, stage):
                        copy.start()

    def product(factor, t):
        return jnp.dot(factor[t], panel[pl.ds(pl.multiple_of(t * tile_rows, tile_rows), tile_rows), :],
                       preferred_element_type=jnp.float32)

    def use(distance):
        for step, t, ok, onward in arrivals(distance):
            @pl.when(ok)
            def _():
                for q in range(chunks):
                    r_waits(t, q, len(bits) - 1)
                total[...] += product(left, t)

    keep_tile.wait()
    for copy in keep_left:
        copy.wait()
    started = False
    for distance in range(1, rows + len(bits)):
        if distance < rows:
            take(distance)
        for stage in range(1, len(bits)):
            if 1 <= distance - stage < rows:
                spread(distance - stage, stage)
        if not started:
            for other in others:
                for part in range(ratio):
                    a_copy(other, other, part).wait_recv()
            total[...] = product(left, z)
            started = True
        if 1 <= distance - len(bits) < rows:
            use(distance - len(bits))

    row_block = (p * own + lax.broadcasted_iota(jnp.int32, (own, block), 0)) // block

    def widen(keep, column):
        wide = jnp.zeros((own, block), jnp.float32)
        for i in range(tile_rows // block):
            wide = jnp.where(row_block == i, keep[i, column].astype(jnp.float32), wide)
        return wide

    per_part = tile_rows // block
    for column in range(tile_cols // block):
        span = pl.ds(column * block, block)
        square = total[:, span] * widen(keep_square, column)
        total[:, span] = square
        low[c * ratio + column // per_part, :, pl.ds(column % per_part * block, block)] = square.astype(jnp.bfloat16)
    for other in others:
        for part in range(ratio):
            l_copy(c, other, part).start()
    cube = product(low, c * ratio)
    for part in range(1, ratio):
        cube = cube + product(low, c * ratio + part)
    out[...] = cube
    for other in others:
        for part in range(ratio):
            l_copy(other, other, part).wait_recv()
            out[...] += product(low, other * ratio + part)
    for column in range(tile_cols // block):
        span = pl.ds(column * block, block)
        out[:, span] = 3.0 * total[:, span] - 2.0 * (out[:, span] * widen(keep_cube, column))

    for q in range(chunks):
        for step, ok in ways:
            @pl.when(ok)
            def _():
                z_copy(z, q, step, True).wait_send()
        for distance in range(1, rows):
            for step, t, ok, onward in arrivals(distance):
                @pl.when(ok)
                def _():
                    @pl.when(onward)
                    def _():
                        z_copy(t, q, step).wait_send()
                    for stage in range(len(bits)):
                        for copy in r_copies(t, q, stage):
                            copy.wait_send()
    for other in others:
        for part in range(ratio):
            a_copy(c, other, part).wait_send()
            l_copy(c, other, part).wait_send()


def mirror(table, rows, cols):
    last = rows - 1
    return {(last - z, cols - 1 - c): [(last - i, last - j) for i, j in blocks]
            for (z, c), blocks in table.items()}


def folded_plan():
    down = {(3, 0): [(3, 1), (3, 0)], (3, 1): [(3, 3)],
            (2, 0): [(2, 1), (3, 1)], (2, 1): [(2, 2), (2, 3), (3, 3)],
            (1, 0): [(1, 1), (2, 1), (3, 1)], (1, 1): [(2, 2), (2, 3), (3, 3)]}
    across = {(0, 1): [(0, 2), (0, 3)], (0, 0): [(2, 1), (3, 1)], (1, 1): [(0, 2), (0, 3)]}
    rows, cols = 4, 2
    up = mirror(down, rows, cols)
    across = {**across, **mirror(across, rows, cols)}
    ready = {(z, c, z, j): 0.0 for z in range(rows) for c in range(cols) for j in (2 * c, 2 * c + 1)}
    links = [((z, c), (z - 1, c), down.get((z, c), [])) for z in range(rows - 1, 0, -1) for c in range(cols)]
    links += [((z, c), (z + 1, c), up.get((z, c), [])) for z in range(rows - 1) for c in range(cols)]
    links += [((z, c), (z, 1 - c), across.get((z, c), [])) for z in range(rows) for c in range(cols)]
    received = {(z, c): [] for z in range(rows) for c in range(cols)}
    for source, target, blocks in links:
        free = 0.0
        for block in blocks:
            free = max(free, ready[source + block]) + 1.0
            ready[target + block] = free + 0.7
            received[target].append((free, block))
    plans = {}
    for z in range(rows):
        for c in range(cols):
            order = [block for _, block in sorted(received[z, c])]
            plans[z, c] = (down.get((z, c), []), up.get((z, c), []), across.get((z, c), []), order)
    return plans


def folded_kernel(rows, cols, reps, block, chunks, density, keep_square, keep_cube, out,
                  full, left, low, total, send, arrive, r_send, r_recv, a_send, a_recv,
                  l_send, l_recv, local_sem):
    tile_rows, tile_cols = density.shape
    own = tile_rows // reps
    piece = own // chunks
    ratio = tile_cols // tile_rows
    z, c, p = lax.axis_index("row"), lax.axis_index("col"), lax.axis_index("rep")
    near, far = reps // 2, 1
    other = 1 - c
    plans = folded_plan()

    barrier = pltpu.get_barrier_semaphore()
    for step, ok in ((1, z < rows - 1), (-1, z > 0)):
        @pl.when(ok)
        def _():
            pl.semaphore_signal(barrier, inc=1, device_id={"row": z + step}, device_id_type=MESH)
    for bit in (near, far):
        pl.semaphore_signal(barrier, inc=1, device_id={"rep": flip(p, bit)}, device_id_type=MESH)
    pl.semaphore_signal(barrier, inc=1, device_id={"col": other}, device_id_type=MESH)
    keep_tile = [
        pltpu.make_async_copy(density.at[:, pl.ds(part * tile_rows, tile_rows)],
                              full.at[z, c * ratio + part], local_sem.at[part])
        for part in range(ratio)
    ]
    own_rows = pl.ds(pl.multiple_of(p * own, own), own)
    keep_left = [
        pltpu.make_async_copy(density.at[own_rows, pl.ds(part * tile_rows, tile_rows)],
                              left.at[c * ratio + part], local_sem.at[ratio + part])
        for part in range(ratio)
    ]
    for copy in keep_tile + keep_left:
        copy.start()
    below, above = (z + rows - 1) // rows, (2 * rows - 2 - z) // rows
    pl.semaphore_wait(barrier, 3 + below + above)

    def span(member, q):
        return pl.ds(pl.multiple_of(member * own + q * piece, piece), piece)

    ways = ({"row": z - 1}, {"row": z + 1}, {"col": other})

    def hop(way, b, q, mine=None, wide=False):
        member = flip(p, near) if wide else p
        target = full.at[b[0], b[1], span(member, q)]
        source = target
        if mine is not None:
            source = density.at[span(member, q), pl.ds(mine * tile_rows, tile_rows)]
        return pltpu.make_async_remote_copy(
            source, target, send.at[3 if wide else way, b[0], b[1], q],
            (r_recv.at[0, b[0], b[1], q] if wide else arrive.at[b[0], b[1], q]),
            device_id=ways[way], device_id_type=MESH)

    def near_copy(b, q, member):
        ref = full.at[b[0], b[1], span(member, q)]
        return pltpu.make_async_remote_copy(
            ref, ref, r_send.at[0, b[0], b[1], q], r_recv.at[0, b[0], b[1], q],
            device_id={"rep": flip(p, near)}, device_id_type=MESH)

    def far_copy(b, q, which, member):
        ref = full.at[b[0], b[1], span(member, q)]
        return pltpu.make_async_remote_copy(
            ref, ref, r_send.at[which, b[0], b[1], q], r_recv.at[which, b[0], b[1], q],
            device_id={"rep": flip(p, far)}, device_id_type=MESH)

    def a_copy(owner, part):
        return pltpu.make_async_remote_copy(
            density.at[own_rows, pl.ds(part * tile_rows, tile_rows)],
            left.at[owner * ratio + part], a_send.at[part], a_recv.at[part],
            device_id={"col": other}, device_id_type=MESH)

    def l_copy(owner, part):
        return pltpu.make_async_remote_copy(
            low.at[owner * ratio + part], low.at[owner * ratio + part],
            l_send.at[part], l_recv.at[part], device_id={"col": other}, device_id_type=MESH)

    class Chip:
        def __init__(self, row, col):
            self.row, self.col = row, col
            self.lists = plans[row, col][:3]
            self.order = plans[row, col][3]
            self.mine = [(row, col * ratio + part) for part in range(ratio)]
            self.theirs = [(row, (1 - col) * ratio + part) for part in range(ratio)]
            self.have = set(self.mine) | set(self.order)
            self.wide_out = [b for b in self.lists[2] if b in self.mine]
            self.wide_in = [b for b in plans[row, 1 - col][2] if b[0] == row and b in self.theirs]
            self.panel_in = len(self.wide_in) == ratio
            self.panel_out = len(self.wide_out) == ratio

        def left(self, k):
            if self.panel_in and (self.row, k) in self.wide_in:
                return full[self.row, k, own_rows, :]
            return left[k]

        def product(self, factor, k, part):
            j = self.col * ratio + part
            if (k, j) in self.have:
                return jnp.dot(factor, full[k, j], preferred_element_type=jnp.float32)
            return lax.dot_general(factor, full[j, k], (((1,), (1,)), ((), ())),
                                   preferred_element_type=jnp.float32)

        def products_of(self, b):
            pairs = []
            if b[1] // ratio == self.col:
                pairs.append((b[0], b[1] % ratio))
            if b[0] // ratio == self.col and (b[1], b[0]) not in self.have:
                pairs.append((b[1], b[0] % ratio))
            return pairs

        def gather(self):
            for q in range(chunks):
                for n in range(3):
                    for way in range(3):
                        if n < len(self.lists[way]) and self.lists[way][n] in self.mine:
                            b = self.lists[way][n]
                            hop(way, b, q, b[1] % ratio).start()
                            if way == 2:
                                hop(way, b, q, b[1] % ratio, True).start()
            if not self.panel_out:
                for part in range(ratio):
                    a_copy(self.col, part).start()
            items = [(b, q) for b in self.order for q in range(chunks)]
            lag = 2
            ready = {b[1] for b in self.mine}
            waiting, seen = [], set()

            def flush():
                for k, part in list(waiting):
                    if k in ready:
                        where = pl.ds(part * tile_rows, tile_rows)
                        value = self.product(self.left(k), k, part)
                        if part in seen:
                            total[:, where] += value
                        else:
                            total[:, where] = value
                            seen.add(part)
                        waiting.remove((k, part))

            for n in range(len(items) + 2 * lag):
                if n < len(items):
                    b, q = items[n]
                    hop(0, b, q).wait_recv()
                    for way in range(3):
                        if b in self.lists[way]:
                            hop(way, b, q).start()
                    if b not in self.wide_in:
                        near_copy(b, q, p).start()
                    far_copy(b, q, 1, p).start()
                    if self.panel_in and b in self.wide_in and q == chunks - 1:
                        ready.add(b[1])
                if 0 <= n - lag < len(items):
                    b, q = items[n - lag]
                    near_copy(b, q, flip(p, near)).wait_recv()
                    far_copy(b, q, 2, flip(p, near)).start()
                if n == 2 * lag:
                    for copy in keep_tile + keep_left:
                        copy.wait()
                    if not self.panel_in:
                        for part in range(ratio):
                            a_copy(1 - self.col, part).wait_recv()
                            ready.add((1 - self.col) * ratio + part)
                    for b in self.mine:
                        waiting += self.products_of(b)
                    flush()
                if 0 <= n - 2 * lag < len(items):
                    b, q = items[n - 2 * lag]
                    far_copy(b, q, 1, flip(p, far)).wait_recv()
                    far_copy(b, q, 2, flip(flip(p, near), far)).wait_recv()
                    if q == chunks - 1:
                        waiting += self.products_of(b)
                        flush()

        def cube(self):
            for part in range(ratio):
                where = pl.ds(part * tile_rows, tile_rows)
                value = self.product(low[self.mine[0][1]], self.mine[0][1], part)
                for b in self.mine[1:]:
                    value = value + self.product(low[b[1]], b[1], part)
                out[:, where] = value
            for number, b in enumerate(self.theirs):
                l_copy(1 - self.col, number).wait_recv()
                for part in range(ratio):
                    where = pl.ds(part * tile_rows, tile_rows)
                    out[:, where] += self.product(low[b[1]], b[1], part)

        def drain(self):
            for q in range(chunks):
                for way in range(3):
                    for b in self.lists[way]:
                        hop(way, b, q).wait_send()
                        if way == 2 and b in self.mine:
                            hop(way, b, q, None, True).wait_send()
                for b in self.order:
                    if b not in self.wide_in:
                        near_copy(b, q, p).wait_send()
                    far_copy(b, q, 1, p).wait_send()
                    far_copy(b, q, 2, flip(p, near)).wait_send()
            if not self.panel_out:
                for part in range(ratio):
                    a_copy(self.col, part).wait_send()

    def each_chip(action):
        for row in range(rows):
            for col in range(cols):
                @pl.when((z == row) & (c == col))
                def _():
                    action(Chip(row, col))

    each_chip(Chip.gather)
    widen = widener(p, own, block, tile_rows)
    per_part = tile_rows // block
    for column in range(tile_cols // block):
        where = pl.ds(column * block, block)
        square = total[:, where] * widen(keep_square, column)
        total[:, where] = square
        low[c * ratio + column // per_part, :, pl.ds(column % per_part * block, block)] = square.astype(jnp.bfloat16)
        if column % per_part == per_part - 1:
            l_copy(c, column // per_part).start()
    each_chip(Chip.cube)
    for column in range(tile_cols // block):
        where = pl.ds(column * block, block)
        out[:, where] = 3.0 * total[:, where] - 2.0 * (out[:, where] * widen(keep_cube, column))
    for part in range(ratio):
        l_copy(c, part).wait_send()
    each_chip(Chip.drain)


def widener(p, own, block, tile_rows):
    row_block = (p * own + lax.broadcasted_iota(jnp.int32, (own, block), 0)) // block

    def widen(keep, column):
        wide = jnp.zeros((own, block), jnp.float32)
        for i in range(tile_rows // block):
            wide = jnp.where(row_block == i, keep[i, column].astype(jnp.float32), wide)
        return wide

    return widen


def local(rows, cols, reps, mat, density, keep_square, keep_cube):
    tile_rows, tile_cols = density.shape
    block = tile_rows // keep_square.shape[0]
    own = tile_rows // reps
    ratio = tile_cols // tile_rows
    chunks = 3 if own % 48 == 0 else 1
    dma = pltpu.SemaphoreType.DMA
    vmem = pltpu.VMEM
    folded = (rows, cols, ratio, reps) == (4, 2, 2, 4)
    body = folded_kernel if folded else kernel
    scratch = [
        vmem((rows, rows, tile_rows, tile_rows), jnp.bfloat16),
        vmem((rows, own, tile_rows), jnp.bfloat16),
        vmem((rows, own, tile_rows), jnp.bfloat16),
        vmem((own, tile_cols), jnp.float32),
        dma((4, rows, rows, chunks)),
        dma((rows, rows, chunks)),
        dma((reps - 1, rows, rows, chunks)),
        dma((reps - 1, rows, rows, chunks)),
        dma((ratio,)),
        dma((ratio,)),
        dma((ratio,)),
        dma((ratio,)),
        dma((2 * ratio,)),
    ]
    return pl.pallas_call(
        functools.partial(body, rows, cols, reps, block, chunks),
        out_shape=pltpu.VMEM((own, tile_cols), jnp.float32),
        in_specs=[
            pl.BlockSpec(memory_space=pl.ANY),
            pl.BlockSpec(memory_space=pltpu.SMEM),
            pl.BlockSpec(memory_space=pltpu.SMEM),
        ],
        out_specs=pl.BlockSpec(memory_space=pltpu.VMEM),
        scratch_shapes=scratch if folded else [
            pltpu.VMEM((mat, tile_cols), jnp.bfloat16),
            pltpu.VMEM((rows, own, tile_rows), jnp.bfloat16),
            pltpu.VMEM((rows, own, tile_rows), jnp.bfloat16),
            pltpu.VMEM((own, tile_cols), jnp.float32),
            dma((2, rows, chunks)),
            dma((rows, chunks)),
            dma((reps - 1, rows, chunks)),
            dma((reps - 1, rows, chunks)),
            dma((cols, ratio)),
            dma((cols, ratio)),
            dma((cols, ratio)),
            dma((cols, ratio)),
            dma((1 + ratio,)),
        ],
        compiler_params=pltpu.CompilerParams(collective_id=0, has_side_effects=True),
    )(density, keep_square, keep_cube)


def solution(mesh):
    rows, cols, reps = (mesh.shape[axis] for axis in ("row", "col", "rep"))

    def body(density, keep_square, keep_cube):
        return local(rows, cols, reps, density.shape[0] * rows, density, keep_square, keep_cube)

    return jax.shard_map(
        body,
        mesh=mesh,
        in_specs=(P("row", "col"), P("row", "col"), P("row", "col")),
        out_specs=P(("row", "rep"), "col"),
        check_vma=False,
    )
```

```python
import functools

import jax
import jax.numpy as jnp
from jax import lax
from jax.experimental import pallas as pl
from jax.experimental.pallas import tpu as pltpu
from jax.sharding import PartitionSpec as P

MESH = pl.DeviceIdType.MESH


def flip(index, bit):
    return index + bit - 2 * bit * (index // bit % 2)


def kernel(rows, cols, reps, block, chunks, density, keep_square, keep_cube, out,
           panel, left, low, total, z_send, z_recv, r_send, r_recv, a_send, a_recv,
           l_send, l_recv, local_sem):
    tile_rows, tile_cols = density.shape
    own = tile_rows // reps
    piece = own // chunks
    ratio = tile_cols // tile_rows
    z, c, p = lax.axis_index("row"), lax.axis_index("col"), lax.axis_index("rep")
    bits = []
    bit = reps // 2
    while bit:
        bits.append(bit)
        bit //= 2
    others = [lax.rem(c + step, cols) for step in range(1, cols)]

    barrier = pltpu.get_barrier_semaphore()
    for step, ok in ((1, z < rows - 1), (-1, z > 0)):
        @pl.when(ok)
        def _():
            pl.semaphore_signal(barrier, inc=1, device_id={"row": z + step}, device_id_type=MESH)
    for bit in bits:
        pl.semaphore_signal(barrier, inc=1, device_id={"rep": flip(p, bit)}, device_id_type=MESH)
    for other in others:
        pl.semaphore_signal(barrier, inc=1, device_id={"col": other}, device_id_type=MESH)
    keep_tile = pltpu.make_async_copy(
        density, panel.at[pl.ds(pl.multiple_of(z * tile_rows, tile_rows), tile_rows)], local_sem.at[0])
    keep_tile.start()
    keep_left = [
        pltpu.make_async_copy(
            density.at[pl.ds(pl.multiple_of(p * own, own), own), pl.ds(part * tile_rows, tile_rows)],
            left.at[c * ratio + part], local_sem.at[1 + part])
        for part in range(ratio)
    ]
    for copy in keep_left:
        copy.start()
    below, above = (z + rows - 1) // rows, (2 * rows - 2 - z) // rows
    pl.semaphore_wait(barrier, len(bits) + len(others) + below + above)

    def slot(t, member, q):
        return panel.at[pl.ds(pl.multiple_of(t * tile_rows + member * own + q * piece, piece), piece)]

    def packed(t, place):
        return t - (t - place - 1 + rows) // rows

    def z_copy(t, q, step, first=False, sending=True):
        at = z if sending else z - step
        source = slot(t, p, q)
        if first:
            source = density.at[pl.ds(pl.multiple_of(p * own + q * piece, piece), piece)]
        return pltpu.make_async_remote_copy(
            source, slot(t, p, q), z_send.at[t + (1 - step) // 2, q],
            z_recv.at[packed(t, at + step), q],
            device_id={"row": z + step}, device_id_type=MESH)

    def r_copies(t, q, stage):
        members = [p]
        for bit in bits[:stage]:
            members = members + [flip(member, bit) for member in members]
        peer = flip(p, bits[stage])
        base = 2 ** stage - 1
        return [
            pltpu.make_async_remote_copy(
                slot(t, member, q), slot(t, member, q), r_send.at[base + i, packed(t, z), q],
                r_recv.at[base + i, packed(t, z), q], device_id={"rep": peer}, device_id_type=MESH)
            for i, member in enumerate(members)
        ]

    def r_waits(t, q, stage):
        peer = flip(p, bits[stage])
        members = [peer]
        for bit in bits[:stage]:
            members = members + [flip(member, bit) for member in members]
        base = 2 ** stage - 1
        for i, member in enumerate(members):
            pltpu.make_async_remote_copy(
                slot(t, member, q), slot(t, member, q), r_send.at[base + i, packed(t, z), q],
                r_recv.at[base + i, packed(t, z), q], device_id={"rep": peer}, device_id_type=MESH).wait_recv()

    def a_copy(owner, peer, part):
        return pltpu.make_async_remote_copy(
            density.at[pl.ds(pl.multiple_of(p * own, own), own), pl.ds(part * tile_rows, tile_rows)],
            left.at[owner * ratio + part], a_send.at[peer, part], a_recv.at[owner, part],
            device_id={"col": peer}, device_id_type=MESH)

    def l_copy(owner, peer, part):
        return pltpu.make_async_remote_copy(
            low.at[owner * ratio + part], low.at[owner * ratio + part],
            l_send.at[peer, part], l_recv.at[owner, part],
            device_id={"col": peer}, device_id_type=MESH)

    ways = ((1, z < rows - 1), (-1, z > 0))
    for q in range(chunks):
        for step, ok in ways:
            @pl.when(ok)
            def _():
                z_copy(z, q, step, True).start()
    for other in others:
        for part in range(ratio):
            a_copy(c, other, part).start()

    def arrivals(distance):
        return ((1, z - distance, z - distance >= 0, z < rows - 1),
                (-1, z + distance, z + distance < rows, z > 0))

    def take(distance):
        for q in range(chunks):
            for step, t, ok, onward in arrivals(distance):
                @pl.when(ok)
                def _():
                    z_copy(t, q, step, sending=False).wait_recv()

                    @pl.when(onward)
                    def _():
                        z_copy(t, q, step).start()
                    for copy in r_copies(t, q, 0):
                        copy.start()

    def spread(distance, stage):
        for q in range(chunks):
            for step, t, ok, onward in arrivals(distance):
                @pl.when(ok)
                def _():
                    r_waits(t, q, stage - 1)
                    for copy in r_copies(t, q, stage):
                        copy.start()

    def product(factor, t):
        return jnp.dot(factor[t], panel[pl.ds(pl.multiple_of(t * tile_rows, tile_rows), tile_rows), :],
                       preferred_element_type=jnp.float32)

    def use(distance):
        for step, t, ok, onward in arrivals(distance):
            @pl.when(ok)
            def _():
                for q in range(chunks):
                    r_waits(t, q, len(bits) - 1)
                total[...] += product(left, t)

    keep_tile.wait()
    for copy in keep_left:
        copy.wait()
    started = False
    for distance in range(1, rows + len(bits)):
        if distance < rows:
            take(distance)
        for stage in range(1, len(bits)):
            if 1 <= distance - stage < rows:
                spread(distance - stage, stage)
        if not started:
            for other in others:
                for part in range(ratio):
                    a_copy(other, other, part).wait_recv()
            total[...] = product(left, z)
            started = True
        if 1 <= distance - len(bits) < rows:
            use(distance - len(bits))

    row_block = (p * own + lax.broadcasted_iota(jnp.int32, (own, block), 0)) // block

    def widen(keep, column):
        wide = jnp.zeros((own, block), jnp.float32)
        for i in range(tile_rows // block):
            wide = jnp.where(row_block == i, keep[i, column].astype(jnp.float32), wide)
        return wide

    per_part = tile_rows // block
    for column in range(tile_cols // block):
        span = pl.ds(column * block, block)
        square = total[:, span] * widen(keep_square, column)
        total[:, span] = square
        low[c * ratio + column // per_part, :, pl.ds(column % per_part * block, block)] = square.astype(jnp.bfloat16)
    for other in others:
        for part in range(ratio):
            l_copy(c, other, part).start()
    cube = product(low, c * ratio)
    for part in range(1, ratio):
        cube = cube + product(low, c * ratio + part)
    out[...] = cube
    for other in others:
        for part in range(ratio):
            l_copy(other, other, part).wait_recv()
            out[...] += product(low, other * ratio + part)
    for column in range(tile_cols // block):
        span = pl.ds(column * block, block)
        out[:, span] = 3.0 * total[:, span] - 2.0 * (out[:, span] * widen(keep_cube, column))

    for q in range(chunks):
        for step, ok in ways:
            @pl.when(ok)
            def _():
                z_copy(z, q, step, True).wait_send()
        for distance in range(1, rows):
            for step, t, ok, onward in arrivals(distance):
                @pl.when(ok)
                def _():
                    @pl.when(onward)
                    def _():
                        z_copy(t, q, step).wait_send()
                    for stage in range(len(bits)):
                        for copy in r_copies(t, q, stage):
                            copy.wait_send()
    for other in others:
        for part in range(ratio):
            a_copy(c, other, part).wait_send()
            l_copy(c, other, part).wait_send()


def local(rows, cols, reps, mat, density, keep_square, keep_cube):
    tile_rows, tile_cols = density.shape
    block = tile_rows // keep_square.shape[0]
    own = tile_rows // reps
    ratio = tile_cols // tile_rows
    chunks = 3 if own % 48 == 0 else 1
    dma = pltpu.SemaphoreType.DMA
    return pl.pallas_call(
        functools.partial(kernel, rows, cols, reps, block, chunks),
        out_shape=pltpu.VMEM((own, tile_cols), jnp.float32),
        in_specs=[
            pl.BlockSpec(memory_space=pl.ANY),
            pl.BlockSpec(memory_space=pltpu.SMEM),
            pl.BlockSpec(memory_space=pltpu.SMEM),
        ],
        out_specs=pl.BlockSpec(memory_space=pltpu.VMEM),
        scratch_shapes=[
            pltpu.VMEM((mat, tile_cols), jnp.bfloat16),
            pltpu.VMEM((rows, own, tile_rows), jnp.bfloat16),
            pltpu.VMEM((rows, own, tile_rows), jnp.bfloat16),
            pltpu.VMEM((own, tile_cols), jnp.float32),
            dma((rows + 1, chunks)),
            dma((rows - 1, chunks)),
            dma((reps - 1, rows - 1, chunks)),
            dma((reps - 1, rows - 1, chunks)),
            dma((cols, ratio)),
            dma((cols, ratio)),
            dma((cols, ratio)),
            dma((cols, ratio)),
            dma((1 + ratio,)),
        ],
        compiler_params=pltpu.CompilerParams(collective_id=0, has_side_effects=True),
    )(density, keep_square, keep_cube)


def solution(mesh):
    rows, cols, reps = (mesh.shape[axis] for axis in ("row", "col", "rep"))

    def body(density, keep_square, keep_cube):
        return local(rows, cols, reps, density.shape[0] * rows, density, keep_square, keep_cube)

    return jax.shard_map(
        body,
        mesh=mesh,
        in_specs=(P("row", "col"), P("row", "col"), P("row", "col")),
        out_specs=P(("row", "rep"), "col"),
        check_vma=False,
    )
```
